32 devices in a mesh: cfg: 1, pair: 16 (over z, y, x), blk: 2 (over core).
Axes of the slice: x: 2, y: 2, z: 4, core: 2. Of those that a mesh axis runs over, the one named last changes fastest.
Arguments:
- elementals: bfloat16 [16, 8, 2, 65536], P('cfg', None, None, ('pair', 'blk')), may hold values from -0.079589844 to 0.079589844
- perambulator: bfloat16 [16, 2, 1024, 1024], P(('cfg', 'pair'), None, None, 'blk'), may hold values from -0.1875 to 0.1875
- pairs: int32 [16, 2], replicated, may hold values from 0 to 15, as said below
- elem_index: int32 [16, 24], replicated, may hold values from 0 to 7
- coef_code: int32 [16, 24, 4, 4], replicated, may hold values from -2 to 2
- term_count: int32 [16], replicated, may hold values from 12 to 24, as said below
Outputs:
- correlator: float32 [16, 2], P(('cfg', 'pair'))
The draws below stay inside these ranges and needn't reach their ends.
Inputs may be any that keep to these rules, and one draw needn't show every extreme that they name: `pairs`: pair p + 8 lists the two timeslices of pair p in reverse order; the two timeslices of a pair differ. `term_count`: some pair uses all 24 terms.
All inputs are finite; a program needn't handle non-finite values.
Results may differ from the reference program's by a relative error of at most 0.0057.
Values may be sent and summed in bfloat16 or wider, within the bound.
No kernel may reach another device: no remote copies, remote signals or barrier semaphores. Data moves between devices by JAX's collectives and lax.ppermute only.
A program may use at most 64 MiB of HBM per device.

```python
import jax
import jax.numpy as jnp
from jax import lax

NV = 256
NS = 4
NOP = 8
NTERM = 24
ORD = 1024
NT = 16
PAIRS = 16


def draw_pairs(key, part):
    key_first, key_step = jax.random.split(jax.random.fold_in(key, 11))
    first = jax.random.randint(key_first, (PAIRS // 2,), 0, NT)
    step = jax.random.randint(key_step, (PAIRS // 2,), 1, NT)
    leading = jnp.arange(PAIRS // 2) == 0
    first = jnp.where(leading, NT - 1, first)
    step = jnp.where(leading, 1, step)
    second = (first + step) % NT
    lower = jnp.stack([first, second], 1)
    upper = jnp.stack([second, first], 1)
    return jnp.concatenate([lower, upper], 0).astype(jnp.int32)


def draw_term_count(key, part):
    key_count, key_where = jax.random.split(jax.random.fold_in(key, 23))
    counts = jax.random.randint(key_count, (PAIRS,), NTERM // 2, NTERM + 1)
    where = jax.random.randint(key_where, (), 0, PAIRS)
    counts = jnp.where(jnp.arange(PAIRS) == where, NTERM, counts)
    return counts.astype(jnp.int32)


def set_ends(result, rng, least, largest):
    extent = result.shape
    place = [jax.random.randint(jax.random.fold_in(rng, axis), (), 0, extent[axis]) for axis in range(len(extent))]
    result = result.at[tuple(place)].set(least)
    longest = extent.index(max(extent))
    place[longest] = (place[longest] + 1) % extent[longest]
    return result.at[tuple(place)].set(largest)


def levels(rng, shape, pieces, low, largest):
    factor_of = 1.0
    for position, parts in pieces:
        heights = jax.random.uniform(jax.random.fold_in(jax.random.fold_in(rng, 6), position), (parts,), jnp.float32, low / len(pieces), largest / len(pieces))
        factor_of = factor_of * jnp.repeat(jnp.exp(heights), shape[position] // parts).reshape((-1,) + (1,) * (len(shape) - 1 - position))
    return factor_of


def noise(rng, shape, scale, most, cuts=(), kind=jnp.bfloat16):
    loudness = levels(rng, shape, cuts, -0.22, 0.18) if cuts else 1.0
    array = jax.random.normal(rng, shape, jnp.float32) * scale * loudness
    return jnp.minimum(jnp.maximum(array, -most), most).astype(kind)


def setup_inputs(seed: int = 0, part: int = 0) -> dict:
    splits = jax.random.split(jax.random.key(seed), 7)
    own_keys = jax.random.split(jax.random.fold_in(splits[6], part), 7)
    return {
        "elementals": noise(own_keys[0], (NT, NOP, 2, NV * NV), 0.01, 0.079589844, ((3, 32),)),
        "perambulator": noise(own_keys[1], (PAIRS, 2, ORD, ORD), ORD ** -0.5, 0.1875, ((0, 16), (3, 2))),
        "pairs": draw_pairs(jax.random.fold_in(splits[6], 71), part),
        "elem_index": set_ends(jax.random.randint(splits[3], (PAIRS, NTERM), 0, NOP), jax.random.fold_in(splits[3], 1), 0, NOP - 1).astype(jnp.int32),
        "coef_code": set_ends(jax.random.randint(splits[4], (PAIRS, NTERM, NS, NS), -2, 3), jax.random.fold_in(splits[4], 1), -2, 2).astype(jnp.int32),
        "term_count": draw_term_count(jax.random.fold_in(splits[6], 71), part),
    }


def dress(elementals, propagator, first, index, codes, count):
    picked = elementals[first][index].reshape(NTERM, 2, NV, NV)
    used = (jnp.arange(NTERM) < count).astype(jnp.float32)
    weights = codes.astype(jnp.float32) * 0.5 * used[:, None, None]
    blocks = jnp.einsum("kab,kcij->caibj", weights, picked.astype(jnp.float32), precision=lax.Precision.HIGHEST)
    blocks = blocks.astype(jnp.bfloat16).reshape(2, ORD, ORD)
    real_part = jnp.dot(blocks[0], propagator[0], preferred_element_type=jnp.float32) - jnp.dot(blocks[1], propagator[1], preferred_element_type=jnp.float32)
    imag_part = jnp.dot(blocks[0], propagator[1], preferred_element_type=jnp.float32) + jnp.dot(blocks[1], propagator[0], preferred_element_type=jnp.float32)
    return jnp.stack([real_part, imag_part]).astype(jnp.bfloat16)


def reference(elementals, perambulator, pairs, elem_index, coef_code, term_count):
    half = PAIRS // 2

    def one_pair(lower):
        upper = lower + half
        dressed_low = dress(elementals, perambulator[lower], pairs[lower, 0], elem_index[lower], coef_code[lower], term_count[lower])
        dressed_up = dress(elementals, perambulator[upper], pairs[upper, 0], elem_index[upper], coef_code[upper], term_count[upper])
        products = jnp.einsum("zrc,ycr->zy", dressed_low.astype(jnp.float32), dressed_up.astype(jnp.float32), precision=lax.Precision.HIGHEST)
        return jnp.stack([products[0, 0] - products[1, 1], products[0, 1] + products[1, 0]])

    values = lax.map(one_pair, jnp.arange(half, dtype=jnp.int32))
    return jnp.concatenate([values, values], 0)
```

```python
import functools

import jax
import jax.numpy as jnp
from jax import lax
from jax.experimental import pallas as pl
from jax.experimental.pallas import tpu as pltpu
from jax.sharding import PartitionSpec as P

F32 = jnp.float32
BF16 = jnp.bfloat16

ANY = pl.BlockSpec(memory_space=pl.ANY)
VMEM = pl.BlockSpec(memory_space=pltpu.VMEM)
SMEM = pl.BlockSpec(memory_space=pltpu.SMEM)


def pick_kernel(index_ref, table_ref, out_ref, held, into, out):
    count = out_ref.shape[0]
    loads = [
        pltpu.make_async_copy(table_ref.at[index_ref[n]], held.at[n], into.at[n])
        for n in range(count)
    ]
    stores = [pltpu.make_async_copy(held.at[n], out_ref.at[n], out.at[n]) for n in range(count)]
    for load in loads:
        load.start()
    for load, store in zip(loads, stores):
        load.wait()
        store.start()
    for store in stores:
        store.wait()


def pick(table, index):
    shape = (index.shape[0], *table.shape[1:])
    return pl.pallas_call(
        pick_kernel,
        out_shape=jax.ShapeDtypeStruct(shape, table.dtype),
        in_specs=[SMEM, ANY],
        out_specs=ANY,
        scratch_shapes=[
            pltpu.VMEM(shape, table.dtype),
            pltpu.SemaphoreType.DMA((shape[0],)),
            pltpu.SemaphoreType.DMA((shape[0],)),
        ],
        name="pick",
    )(index, table)


def sort_kernel(half, rows, nv, prop_ref, out_ref):
    columns = prop_ref.shape[-1]
    wide = columns // nv
    quarter = nv // 4
    source = lax.broadcasted_iota(jnp.int32, (columns, columns), 0)
    target = lax.broadcasted_iota(jnp.int32, (columns, columns), 1)
    place = lax.rem(target, quarter)
    b = lax.rem(target // quarter, wide)
    side = lax.rem(target // (quarter * wide), 2)
    core = target // (2 * quarter * wide)
    device = side * half + place // rows
    wanted = b * nv + (device * 2 + core) * rows + lax.rem(place, rows)
    order = jnp.where(source == wanted, 1.0, 0.0).astype(BF16)
    for c in range(2):
        out_ref[c] = jnp.dot(prop_ref[c], order, preferred_element_type=F32).astype(BF16)


def dress_kernel(
    ns, where_ref, weight_ref, elem_ref, own_ref, other_ref, *refs
):
    outs, (phi, dressed) = refs[:4], refs[4:]
    nop, _, rows, nv = elem_ref.shape
    step = 16
    chunks = rows // step

    def combine(n, carry):
        c = n // chunks
        first = pl.multiple_of((n % chunks) * step, step)
        parts = [elem_ref[o, c, pl.ds(first, step), :].astype(F32) for o in range(nop)]
        for a in range(ns):
            for b in range(ns):
                total = weight_ref[a * ns + b] * parts[0]
                for o in range(1, nop):
                    total += weight_ref[(o * ns + a) * ns + b] * parts[o]
                phi[c, pl.ds(a * rows + first, step), b * nv : (b + 1) * nv] = total.astype(BF16)
        return carry

    lax.fori_loop(0, 2 * chunks, combine, 0)
    width = dressed.shape[-1]
    core = where_ref[4]
    for prop_ref, place in ((own_ref, core), (other_ref, 1 - core)):
        for group in range(2):
            span = slice(group * 2 * width, (group + 1) * 2 * width)
            prop_real, prop_imag = prop_ref[0, :, span], prop_ref[1, :, span]
            real = jnp.dot(phi[0], prop_real, preferred_element_type=F32) - jnp.dot(
                phi[1], prop_imag, preferred_element_type=F32
            )
            imag = jnp.dot(phi[0], prop_imag, preferred_element_type=F32) + jnp.dot(
                phi[1], prop_real, preferred_element_type=F32
            )
            for side in range(2):
                part = slice(side * width, (side + 1) * width)
                dressed[side * 2 + group, place, 0] = real[:, part].astype(BF16)
                dressed[side * 2 + group, place, 1] = imag[:, part].astype(BF16)
    for n, out in enumerate(outs):
        out[...] = dressed[where_ref[n]]


def dress(where, weight, elem, own, other, ns):
    nop, _, rows, nv = elem.shape
    order = own.shape[1]
    width = order // 8
    block = (2, 2, ns * rows, width)
    return pl.pallas_call(
        functools.partial(dress_kernel, ns),
        out_shape=[jax.ShapeDtypeStruct(block, BF16)] * 4,
        in_specs=[SMEM, SMEM, VMEM, VMEM, VMEM],
        out_specs=[VMEM] * 4,
        scratch_shapes=[
            pltpu.VMEM((2, ns * rows, order), BF16),
            pltpu.VMEM((4, *block), BF16),
        ],
        cost_estimate=pl.CostEstimate(
            flops=16 * ns * rows * order * order // 2,
            bytes_accessed=8 * order * order,
            transcendentals=0,
        ),
        name="dress",
    )(where, weight, elem, own, other)


def trace_kernel(mine_ref, theirs_ref, before_ref, out_ref):
    width = mine_ref.shape[-1]
    real = imag = None
    for block in range(2):
        span = slice(block * width, (block + 1) * width)
        left = [
            jnp.concatenate([mine_ref[0, c, span, :], mine_ref[1, c, span, :]], axis=1)
            for c in range(2)
        ]
        right = [theirs_ref[block, c] for c in range(2)]
        dot = functools.partial(jnp.dot, preferred_element_type=F32)
        re = dot(left[0], right[0]) - dot(left[1], right[1])
        im = dot(left[0], right[1]) + dot(left[1], right[0])
        real = re if real is None else real + re
        imag = im if imag is None else imag + im
    shape = real.shape
    diagonal = lax.broadcasted_iota(jnp.int32, shape, 0) == lax.broadcasted_iota(jnp.int32, shape, 1)
    real = jnp.sum(jnp.where(diagonal, real, 0.0))
    imag = jnp.sum(jnp.where(diagonal, imag, 0.0))
    lane = lax.broadcasted_iota(jnp.int32, out_ref.shape, 1)
    out_ref[...] = before_ref[...] + jnp.where(lane == 0, real, jnp.where(lane == 1, imag, 0.0))


def trace(mine, theirs, before):
    return pl.pallas_call(
        trace_kernel,
        out_shape=jax.ShapeDtypeStruct(before.shape, F32),
        in_specs=[VMEM] * 3,
        out_specs=VMEM,
        cost_estimate=pl.CostEstimate(
            flops=8 * mine.shape[2] ** 3, bytes_accessed=4 * mine.size, transcendentals=0
        ),
        name="trace",
    )(mine, theirs, before)


def shards(elementals, perambulator, pairs, elem_index, coef_code, term_count):
    peers = lax.axis_size("pair")
    half = peers // 2
    me, core = lax.axis_index("pair"), lax.axis_index("blk")
    side = me // half
    nop, entries = elementals.shape[1], elementals.shape[-1]
    nterms, ns = elem_index.shape[1], coef_code.shape[-1]
    order, columns = perambulator.shape[2:]
    nv = order // ns
    rows = entries // nv

    def across(value, turn):
        moves = []
        for p in range(peers):
            for c in range(2):
                moves.append((p * 2 + c, (p + half) % peers * 2 + (c ^ turn[p // half])))
        return lax.ppermute(value, ("pair", "blk"), moves)

    def within(value):
        groups = [list(range(half)), list(range(half, peers))]
        return lax.all_to_all(value, "pair", 0, 0, axis_index_groups=groups, tiled=True)

    times = pairs[:, 0]
    away = pick(elementals, lax.dynamic_slice(times, ((1 - side) * half,), (half,)))
    crossed = across(away, (0, 0))
    home = pick(elementals, lax.dynamic_slice(times, (side * half,), (half,)))

    own = pl.pallas_call(
        functools.partial(sort_kernel, half, rows, nv),
        out_shape=jax.ShapeDtypeStruct(perambulator.shape[1:], BF16),
        in_specs=[VMEM],
        out_specs=VMEM,
        name="sort",
    )(perambulator[0])
    other = lax.ppermute(own, "blk", [(0, 1), (1, 0)])

    used = jnp.arange(nterms) < term_count[me]
    weights = jnp.where(used[:, None, None], coef_code[me], 0)
    named = elem_index[me][None, :] == jnp.arange(nop)[:, None]
    weight = jnp.sum(jnp.where(named[:, :, None, None], weights[None], 0), axis=1)
    weight = (weight.astype(F32) * 0.5).reshape(-1)

    def rows_of(received):
        shaped = received.reshape(half, nop, 2, rows, nv)
        return shaped.transpose(1, 2, 0, 3, 4).reshape(nop, 2, half * rows, nv)

    swap = core ^ side
    where = jnp.stack([side * 2 + core, side * 2 + 1 - core, (1 - side) * 2 + swap, (1 - side) * 2 + 1 - swap, core])
    near, near_turned, mixed, mixed_kept = dress(where, weight, rows_of(within(home)), own, other, ns)
    got_near = across(near, (0, 0))
    got_near_turned = across(near_turned, (1, 1))
    got_mixed = across(mixed, (0, 1))

    where = jnp.stack([side * 2 + swap, side * 2 + 1 - swap, (1 - side) * 2 + core, (1 - side) * 2 + 1 - core, core])
    last, last_kept, far, far_turned = dress(where, weight, rows_of(within(crossed)), own, other, ns)
    got_last = across(last, (0, 1))

    total = jnp.zeros((8, 128), F32)
    total = trace(far, got_near, total)
    total = trace(far_turned, got_near_turned, total)
    total = trace(mixed_kept, got_mixed, total)
    total = trace(last_kept, got_last, total)

    beside = lax.ppermute(total, "blk", [(0, 1), (1, 0)])
    there = across(total, (0, 0))
    there_beside = across(total, (1, 1))
    total = (total + beside) + (there + there_beside)
    return total[:1, :2]


def solution(mesh):
    return jax.shard_map(
        shards,
        mesh=mesh,
        in_specs=(
            P("cfg", None, None, ("pair", "blk")),
            P(("cfg", "pair"), None, None, "blk"),
            P(),
            P(),
            P(),
            P(),
        ),
        out_specs=P(("cfg", "pair"), None),
        check_vma=False,
    )
```

```python
import functools
import math

import jax
import jax.numpy as jnp
from jax import lax
from jax.experimental import pallas as pl
from jax.experimental.pallas import tpu as pltpu
from jax.sharding import PartitionSpec as P


F32 = jnp.float32
BF16 = jnp.bfloat16
MIB = 1 << 20

VMEM = pl.BlockSpec(memory_space=pltpu.VMEM)
SMEM = pl.BlockSpec(memory_space=pltpu.SMEM)


def pick_kernel(here, times_ref, table_ref, out_ref, arrived):
    count = out_ref.shape[0]
    side = lax.axis_index("pair") // count
    first = (side if here else 1 - side) * count
    loads = [
        pltpu.make_async_copy(table_ref.at[times_ref[0, first + n]], out_ref.at[n], arrived.at[n])
        for n in range(count)
    ]
    for load in loads:
        load.start()
    for load in loads:
        load.wait()


def pick(table, times, count, here):
    shape = (count, *table.shape[1:])
    return pl.pallas_call(
        functools.partial(pick_kernel, here),
        out_shape=jax.ShapeDtypeStruct(shape, table.dtype),
        in_specs=[SMEM, pl.BlockSpec(memory_space=pltpu.MemorySpace.HBM)],
        out_specs=VMEM,
        scratch_shapes=[pltpu.SemaphoreType.DMA((count,))],
        compiler_params=pltpu.CompilerParams(vmem_limit_bytes=4 * MIB),
        cost_estimate=pl.CostEstimate(
            flops=0, bytes_accessed=4 * math.prod(shape), transcendentals=0
        ),
        name="pick_home" if here else "pick_away",
    )(times, table)


def sort_kernel(half, rows, nv, prop_ref, out_ref):
    columns = prop_ref.shape[-1]
    wide = columns // nv
    quarter = nv // 4
    source = lax.broadcasted_iota(jnp.int32, (columns, columns), 0)
    target = lax.broadcasted_iota(jnp.int32, (columns, columns), 1)
    place = lax.rem(target, quarter)
    b = lax.rem(target // quarter, wide)
    side = lax.rem(target // (quarter * wide), 2)
    core = target // (2 * quarter * wide)
    device = side * half + place // rows
    wanted = b * nv + (device * 2 + core) * rows + lax.rem(place, rows)
    order = jnp.where(source == wanted, 1.0, 0.0).astype(BF16)
    for c in range(2):
        out_ref[c] = jnp.dot(prop_ref[c], order, preferred_element_type=F32).astype(BF16)


def dress_kernel(
    ns, late, weight_ref, elem_ref, own_ref, other_ref, *refs
):
    core = lax.axis_index("blk")
    side = lax.axis_index("pair") // (lax.axis_size("pair") // 2)
    swap = core ^ side
    if late:
        where = (side, swap), (side, 1 - swap), (1 - side, core), (1 - side, 1 - core)
    else:
        where = (side, core), (side, 1 - core), (1 - side, swap), (1 - side, 1 - swap)
    outs, (phi, dressed) = refs[:4], refs[4:]
    nop, _, rows, nv = elem_ref.shape
    step = 16
    chunks = rows // step

    def combine(n, carry):
        c = n // chunks
        first = pl.multiple_of((n % chunks) * step, step)
        parts = [elem_ref[o, c, pl.ds(first, step), :].astype(F32) for o in range(nop)]
        for a in range(ns):
            for b in range(ns):
                total = weight_ref[a * ns + b] * parts[0]
                for o in range(1, nop):
                    total += weight_ref[(o * ns + a) * ns + b] * parts[o]
                phi[c, pl.ds(a * rows + first, step), b * nv : (b + 1) * nv] = total.astype(BF16)
        return carry

    lax.fori_loop(0, 2 * chunks, combine, 0)
    width = dressed.shape[-1]
    for prop_ref, place in ((own_ref, core), (other_ref, 1 - core)):
        for group in range(2):
            span = slice(group * 2 * width, (group + 1) * 2 * width)
            prop_real, prop_imag = prop_ref[0, :, span], prop_ref[1, :, span]
            real = jnp.dot(phi[0], prop_real, preferred_element_type=F32) - jnp.dot(
                phi[1], prop_imag, preferred_element_type=F32
            )
            imag = jnp.dot(phi[0], prop_imag, preferred_element_type=F32) + jnp.dot(
                phi[1], prop_real, preferred_element_type=F32
            )
            for side in range(2):
                part = slice(side * width, (side + 1) * width)
                dressed[side * 2 + group, place, 0] = real[:, part].astype(BF16)
                dressed[side * 2 + group, place, 1] = imag[:, part].astype(BF16)
    for (s, c), out in zip(where, outs):
        out[...] = dressed[s * 2 + c]


def dress(late, weight, elem, own, other, ns):
    _, _, rows, _ = elem.shape
    order = own.shape[1]
    width = order // 8
    block = (2, 2, ns * rows, width)
    return pl.pallas_call(
        functools.partial(dress_kernel, ns, late),
        out_shape=[jax.ShapeDtypeStruct(block, BF16)] * 4,
        in_specs=[SMEM, VMEM, VMEM, VMEM],
        out_specs=[VMEM] * 4,
        scratch_shapes=[
            pltpu.VMEM((2, ns * rows, order), BF16),
            pltpu.VMEM((4, *block), BF16),
        ],
        cost_estimate=pl.CostEstimate(
            flops=16 * ns * rows * order * order // 2,
            bytes_accessed=8 * order * order,
            transcendentals=0,
        ),
        compiler_params=pltpu.CompilerParams(vmem_limit_bytes=20 * MIB),
        name="dress_late" if late else "dress_early",
    )(weight, elem, own, other)


def trace_kernel(mine_ref, theirs_ref, before_ref, out_ref):
    width = mine_ref.shape[-1]
    real = imag = None
    for block in range(2):
        span = slice(block * width, (block + 1) * width)
        left = [
            jnp.concatenate([mine_ref[0, c, span, :], mine_ref[1, c, span, :]], axis=1)
            for c in range(2)
        ]
        right = [theirs_ref[block, c] for c in range(2)]
        dot = functools.partial(jnp.dot, preferred_element_type=F32)
        re = dot(left[0], right[0]) - dot(left[1], right[1])
        im = dot(left[0], right[1]) + dot(left[1], right[0])
        real = re if real is None else real + re
        imag = im if imag is None else imag + im
    shape = real.shape
    diagonal = lax.broadcasted_iota(jnp.int32, shape, 0) == lax.broadcasted_iota(jnp.int32, shape, 1)
    real = jnp.sum(jnp.where(diagonal, real, 0.0))
    imag = jnp.sum(jnp.where(diagonal, imag, 0.0))
    lane = lax.broadcasted_iota(jnp.int32, out_ref.shape, 1)
    out_ref[...] = before_ref[...] + jnp.where(lane == 0, real, jnp.where(lane == 1, imag, 0.0))


def trace(mine, theirs, before):
    return pl.pallas_call(
        trace_kernel,
        out_shape=jax.ShapeDtypeStruct(before.shape, F32),
        in_specs=[VMEM] * 3,
        out_specs=VMEM,
        cost_estimate=pl.CostEstimate(
            flops=8 * mine.shape[2] ** 3, bytes_accessed=4 * mine.size, transcendentals=0
        ),
        compiler_params=pltpu.CompilerParams(vmem_limit_bytes=4 * MIB),
        name="trace",
    )(mine, theirs, before)


def shards(elementals, perambulator, pairs, elem_index, coef_code, term_count):
    peers = lax.axis_size("pair")
    half = peers // 2
    me = lax.axis_index("pair")
    nop, entries = elementals.shape[1], elementals.shape[-1]
    nterms, ns = elem_index.shape[1], coef_code.shape[-1]
    order, columns = perambulator.shape[2:]
    nv = order // ns
    rows = entries // nv

    def across(value, turn):
        moves = []
        for p in range(peers):
            for c in range(2):
                moves.append((p * 2 + c, (p + half) % peers * 2 + (c ^ turn[p // half])))
        return lax.ppermute(value, ("pair", "blk"), moves)

    def beside(value):
        return lax.ppermute(value, "blk", [(0, 1), (1, 0)])

    def within(value):
        groups = [list(range(half)), list(range(half, peers))]
        return lax.all_to_all(value, "pair", 0, 0, axis_index_groups=groups, tiled=True)

    def rows_of(received):
        shaped = received.reshape(half, nop, 2, rows, nv)
        return shaped.transpose(1, 2, 0, 3, 4).reshape(nop, 2, half * rows, nv)

    times = pairs.T
    crossed = across(pick(elementals, times, half, False), (0, 0))
    home = within(pick(elementals, times, half, True))

    own = pl.pallas_call(
        functools.partial(sort_kernel, half, rows, nv),
        out_shape=jax.ShapeDtypeStruct(perambulator.shape[1:], BF16),
        in_specs=[VMEM],
        out_specs=VMEM,
        compiler_params=pltpu.CompilerParams(vmem_limit_bytes=16 * MIB),
        cost_estimate=pl.CostEstimate(
            flops=4 * order * columns**2, bytes_accessed=8 * order * columns, transcendentals=0
        ),
        name="sort",
    )(perambulator[0])
    other = beside(own)

    used = jnp.arange(nterms) < term_count[me]
    weights = jnp.where(used[:, None, None], coef_code[me], 0)
    named = elem_index[me][None, :] == jnp.arange(nop)[:, None]
    weight = jnp.sum(jnp.where(named[:, :, None, None], weights[None], 0), axis=1)
    weight = (weight.astype(F32) * 0.5).reshape(-1)

    near, near_turned, mixed, mixed_kept = dress(False, weight, rows_of(home), own, other, ns)
    got_near = across(near, (0, 0))
    got_near_turned = across(near_turned, (1, 1))
    got_mixed = across(mixed, (0, 1))

    away = within(crossed)
    last, last_kept, far, far_turned = dress(True, weight, rows_of(away), own, other, ns)
    got_last = across(last, (0, 1))

    total = jnp.zeros((8, 128), F32)
    total = trace(far, got_near, total)
    total = trace(far_turned, got_near_turned, total)
    total = trace(mixed_kept, got_mixed, total)
    total = trace(last_kept, got_last, total)

    total = (total + beside(total)) + (across(total, (0, 0)) + across(total, (1, 1)))
    return total[:1, :2]


def solution(mesh):
    return jax.shard_map(
        shards,
        mesh=mesh,
        in_specs=(
            P("cfg", None, None, ("pair", "blk")),
            P(("cfg", "pair"), None, None, "blk"),
            P(),
            P(),
            P(),
            P(),
        ),
        out_specs=P(("cfg", "pair"), None),
        check_vma=False,
    )
```

```python
import functools

import jax
import jax.numpy as jnp
from jax import lax
from jax.experimental import pallas as pl
from jax.experimental.pallas import tpu as pltpu
from jax.sharding import PartitionSpec as P


F32 = jnp.float32
BF16 = jnp.bfloat16
MIB = 1 << 20

ANY = pl.BlockSpec(memory_space=pl.ANY)
VMEM = pl.BlockSpec(memory_space=pltpu.VMEM)
SMEM = pl.BlockSpec(memory_space=pltpu.SMEM)


def pick_kernel(few, times_ref, table_ref, few_ref, rest_ref, home_ref, left):
    half = home_ref.shape[0]
    side = lax.axis_index("pair") // half
    stores = []
    for n in range(2 * half):
        pair = ((1 - side) * half + n) if n < half else (side * half + n - half)
        out = few_ref.at[n] if n < few else rest_ref.at[n - few] if n < half else home_ref.at[n - half]
        stores.append(pltpu.make_async_copy(table_ref.at[times_ref[0, pair]], out, left.at[n]))
    for store in stores:
        store.start()
    for store in stores:
        store.wait()


def pick(table, times, few, half):
    counts = (few, half - few, half)
    return pl.pallas_call(
        functools.partial(pick_kernel, few),
        out_shape=[jax.ShapeDtypeStruct((n, *table.shape[1:]), table.dtype) for n in counts],
        in_specs=[SMEM, VMEM],
        out_specs=[ANY] * 3,
        scratch_shapes=[pltpu.SemaphoreType.DMA((2 * half,))],
        cost_estimate=pl.CostEstimate(
            flops=0, bytes_accessed=4 * table.size, transcendentals=0
        ),
        name="pick",
    )(times, table)


def sort_kernel(half, rows, nv, prop_ref, out_ref):
    columns = prop_ref.shape[-1]
    wide = columns // nv
    quarter = nv // 4
    source = lax.broadcasted_iota(jnp.int32, (columns, columns), 0)
    target = lax.broadcasted_iota(jnp.int32, (columns, columns), 1)
    place = lax.rem(target, quarter)
    b = lax.rem(target // quarter, wide)
    side = lax.rem(target // (quarter * wide), 2)
    core = target // (2 * quarter * wide)
    device = side * half + place // rows
    wanted = b * nv + (device * 2 + core) * rows + lax.rem(place, rows)
    order = jnp.where(source == wanted, 1.0, 0.0).astype(BF16)
    width = out_ref.shape[-1]
    for c in range(2):
        sorted_part = jnp.dot(prop_ref[c], order, preferred_element_type=F32).astype(BF16)
        for tile in range(4):
            out_ref[tile, c] = sorted_part[:, tile * width : (tile + 1) * width]


def sort(half, rows, nv, prop):
    _, order, columns = prop.shape
    return pl.pallas_call(
        functools.partial(sort_kernel, half, rows, nv),
        out_shape=jax.ShapeDtypeStruct((4, 2, order, columns // 4), BF16),
        in_specs=[VMEM],
        out_specs=VMEM,
        compiler_params=pltpu.CompilerParams(vmem_limit_bytes=16 * MIB),
        cost_estimate=pl.CostEstimate(
            flops=4 * order * columns**2, bytes_accessed=8 * order * columns, transcendentals=0
        ),
        name="sort",
    )(prop)


def combine(ns, weight_ref, elem_ref, phi_ref):
    nop, _, rows, nv = elem_ref.shape
    span = weight_ref.shape[1] // nop
    shape = (span, nop * span)
    unit = lax.rem(lax.broadcasted_iota(jnp.int32, shape, 1), span) == lax.broadcasted_iota(jnp.int32, shape, 0)
    spread = jnp.concatenate(
        [jnp.where(unit, weight_ref[n : n + 1, :], 0.0).astype(BF16) for n in range(ns * ns)], axis=0
    )
    for c in range(2):
        for first in range(0, rows, span):
            parts = jnp.concatenate([elem_ref[o, c, first : first + span, :] for o in range(nop)], axis=0)
            total = jnp.dot(spread, parts, preferred_element_type=F32).astype(BF16)
            for n in range(ns * ns):
                row = n // ns * rows + first
                phi_ref[c, row : row + span, n % ns * nv : (n % ns + 1) * nv] = total[n * span : (n + 1) * span]


def tiles_of(stage):
    core = lax.axis_index("blk")
    side = lax.axis_index("pair") // (lax.axis_size("pair") // 2)
    swap = core ^ side
    if stage == "early":
        return (side, core), (side, 1 - core), (1 - side, swap), (1 - side, 1 - swap)
    return (side, swap), (side, 1 - swap), (1 - side, core), (1 - side, 1 - core)


def dress_kernel(ns, stage, *refs):
    weight_ref, elem_ref, own_ref, other_ref, *outs, phi = refs[:-2]
    held, arrived = refs[-2:]
    core = lax.axis_index("blk")
    loads = []
    for n, (s, c) in enumerate(tiles_of(stage)):
        pair = [
            pltpu.make_async_copy(ref.at[c * 2 + s], held.at[n, place], arrived.at[n, m])
            for m, (ref, place) in enumerate(((own_ref, core), (other_ref, 1 - core)))
        ]
        for load in pair:
            load.start()
        loads.append(pair)
    combine(ns, weight_ref, elem_ref, phi)
    width = held.shape[-1]
    dot = functools.partial(jnp.dot, preferred_element_type=F32)
    for n, out in enumerate(outs):
        for load in loads[n]:
            load.wait()
        prop_real, prop_imag = (
            jnp.concatenate([held[n, 0, c], held[n, 1, c]], axis=1) for c in range(2)
        )
        real = dot(phi[0], prop_real) - dot(phi[1], prop_imag)
        imag = dot(phi[0], prop_imag) + dot(phi[1], prop_real)
        for place in range(2):
            part = slice(place * width, (place + 1) * width)
            out[place, 0] = real[:, part].astype(BF16)
            out[place, 1] = imag[:, part].astype(BF16)


def dress(stage, weight, elem, own, other, ns):
    order, width = own.shape[2:]
    rows = ns * elem.shape[2]
    block = jax.ShapeDtypeStruct((2, 2, rows, width), BF16)
    return pl.pallas_call(
        functools.partial(dress_kernel, ns, stage),
        out_shape=[block] * 4,
        in_specs=[VMEM, VMEM, ANY, ANY],
        out_specs=[VMEM] * 4,
        scratch_shapes=[
            pltpu.VMEM((2, rows, order), BF16),
            pltpu.VMEM((4, 2, *own.shape[1:]), BF16),
            pltpu.SemaphoreType.DMA((4, 2)),
        ],
        cost_estimate=pl.CostEstimate(
            flops=64 * rows * order * width,
            bytes_accessed=32 * order * width,
            transcendentals=0,
        ),
        compiler_params=pltpu.CompilerParams(vmem_limit_bytes=16 * MIB),
    )(weight, elem, own, other)


def trace_kernel(mine_ref, theirs_ref, before_ref, out_ref):
    width = mine_ref.shape[-1]
    real = imag = None
    for block in range(2):
        span = slice(block * width, (block + 1) * width)
        left = [
            jnp.concatenate([mine_ref[0, c, span, :], mine_ref[1, c, span, :]], axis=1)
            for c in range(2)
        ]
        right = [theirs_ref[block, c] for c in range(2)]
        dot = functools.partial(jnp.dot, preferred_element_type=F32)
        re = dot(left[0], right[0]) - dot(left[1], right[1])
        im = dot(left[0], right[1]) + dot(left[1], right[0])
        real = re if real is None else real + re
        imag = im if imag is None else imag + im
    shape = real.shape
    diagonal = lax.broadcasted_iota(jnp.int32, shape, 0) == lax.broadcasted_iota(jnp.int32, shape, 1)
    real = jnp.sum(jnp.where(diagonal, real, 0.0))
    imag = jnp.sum(jnp.where(diagonal, imag, 0.0))
    lane = lax.broadcasted_iota(jnp.int32, out_ref.shape, 1)
    out_ref[...] = before_ref[...] + jnp.where(lane == 0, real, jnp.where(lane == 1, imag, 0.0))


def trace(mine, theirs, before):
    return pl.pallas_call(
        trace_kernel,
        out_shape=jax.ShapeDtypeStruct(before.shape, F32),
        in_specs=[VMEM] * 3,
        out_specs=VMEM,
        cost_estimate=pl.CostEstimate(
            flops=8 * mine.shape[2] ** 3, bytes_accessed=4 * mine.size, transcendentals=0
        ),
        compiler_params=pltpu.CompilerParams(vmem_limit_bytes=4 * MIB),
        name="trace",
    )(mine, theirs, before)


def shards(elementals, perambulator, pairs, elem_index, coef_code, term_count):
    peers = lax.axis_size("pair")
    half = peers // 2
    me = lax.axis_index("pair")
    nop, entries = elementals.shape[1], elementals.shape[-1]
    nterms, ns = elem_index.shape[1], coef_code.shape[-1]
    order, _ = perambulator.shape[2:]
    nv = order // ns
    rows = entries // nv

    def across(value, turn):
        moves = []
        for p in range(peers):
            for c in range(2):
                moves.append((p * 2 + c, (p + half) % peers * 2 + (c ^ turn[p // half])))
        return lax.ppermute(value, ("pair", "blk"), moves)

    def beside(value):
        return lax.ppermute(value, "blk", [(0, 1), (1, 0)])

    def within(value):
        groups = [list(range(half)), list(range(half, peers))]
        return lax.all_to_all(value, "pair", 0, 0, axis_index_groups=groups, tiled=True)

    def rows_of(received):
        shaped = received.reshape(half, nop, 2, rows, nv)
        return shaped.transpose(1, 2, 0, 3, 4).reshape(nop, 2, half * rows, nv)

    times = pairs.T
    few = max(half // 4, 1)
    away_few, away_rest, home = pick(elementals, times, few, half)
    crossed_few = across(away_few, (0, 0))
    home = within(home)
    crossed_rest = across(away_rest, (0, 0))

    own = sort(half, rows, nv, perambulator[0])
    other = beside(own)

    used = jnp.arange(nterms) < term_count[me]
    weights = jnp.where(used[:, None, None], coef_code[me], 0)
    named = elem_index[me][None, :] == jnp.arange(nop)[:, None]
    weight = jnp.sum(jnp.where(named[:, :, None, None], weights[None], 0), axis=1)
    weight = (weight.astype(F32) * 0.5).reshape(nop, ns * ns).T
    weight = jnp.repeat(weight, nv // nop, axis=1)

    near, near_turned, mixed, mixed_kept = dress("early", weight, rows_of(home), own, other, ns)
    got_near = across(near, (0, 0))
    got_near_turned = across(near_turned, (1, 1))
    crossed = jnp.concatenate([crossed_few, crossed_rest])
    away = within(crossed)
    got_mixed = across(mixed, (0, 1))

    last, last_kept, far, far_turned = dress("late", weight, rows_of(away), own, other, ns)
    got_last = across(last, (0, 1))

    total = jnp.zeros((1, 2), F32)
    total = trace(far, got_near, total)
    total = trace(far_turned, got_near_turned, total)
    total = trace(mixed_kept, got_mixed, total)
    total = trace(last_kept, got_last, total)

    total += across(total, (0, 0))
    return total + beside(total)


def solution(mesh):
    return jax.shard_map(
        shards,
        mesh=mesh,
        in_specs=(
            P("cfg", None, None, ("pair", "blk")),
            P(("cfg", "pair"), None, None, "blk"),
            P(),
            P(),
            P(),
            P(),
        ),
        out_specs=P(("cfg", "pair"), None),
        check_vma=False,
    )
```

```python
import functools

import jax
import jax.numpy as jnp
from jax import lax
from jax.experimental import pallas as pl
from jax.experimental.pallas import tpu as pltpu
from jax.sharding import PartitionSpec as P


F32 = jnp.float32
BF16 = jnp.bfloat16
MIB = 1 << 20

ANY = pl.BlockSpec(memory_space=pl.ANY)
VMEM = pl.BlockSpec(memory_space=pltpu.VMEM)
SMEM = pl.BlockSpec(memory_space=pltpu.SMEM)


def pick_kernel(times_ref, table_ref, away_ref, home_ref, left):
    half = home_ref.shape[0]
    side = lax.axis_index("pair") // half
    stores = []
    for out, first in ((away_ref, (1 - side) * half), (home_ref, side * half)):
        for n in range(half):
            time = times_ref[0, first + n]
            stores.append(pltpu.make_async_copy(table_ref.at[time], out.at[n], left.at[len(stores)]))
    for store in stores:
        store.start()
    for store in stores:
        store.wait()


def pick(table, times, half):
    return pl.pallas_call(
        pick_kernel,
        out_shape=[jax.ShapeDtypeStruct((half, *table.shape[1:]), table.dtype)] * 2,
        in_specs=[SMEM, VMEM],
        out_specs=[ANY] * 2,
        scratch_shapes=[pltpu.SemaphoreType.DMA((2 * half,))],
        cost_estimate=pl.CostEstimate(
            flops=0, bytes_accessed=4 * table.size, transcendentals=0
        ),
        name="pick",
    )(times, table)


def sort_kernel(half, rows, nv, prop_ref, out_ref):
    columns = prop_ref.shape[-1]
    wide = columns // nv
    quarter = nv // 4
    source = lax.broadcasted_iota(jnp.int32, (columns, columns), 0)
    target = lax.broadcasted_iota(jnp.int32, (columns, columns), 1)
    place = lax.rem(target, quarter)
    b = lax.rem(target // quarter, wide)
    side = lax.rem(target // (quarter * wide), 2)
    core = target // (2 * quarter * wide)
    device = side * half + place // rows
    wanted = b * nv + (device * 2 + core) * rows + lax.rem(place, rows)
    order = jnp.where(source == wanted, 1.0, 0.0).astype(BF16)
    width = out_ref.shape[-1]
    for c in range(2):
        sorted_part = jnp.dot(prop_ref[c], order, preferred_element_type=F32).astype(BF16)
        for tile in range(4):
            out_ref[tile, c] = sorted_part[:, tile * width : (tile + 1) * width]


def sort(half, rows, nv, prop):
    _, order, columns = prop.shape
    return pl.pallas_call(
        functools.partial(sort_kernel, half, rows, nv),
        out_shape=jax.ShapeDtypeStruct((4, 2, order, columns // 4), BF16),
        in_specs=[VMEM],
        out_specs=VMEM,
        cost_estimate=pl.CostEstimate(
            flops=4 * order * columns**2, bytes_accessed=8 * order * columns, transcendentals=0
        ),
        name="sort",
    )(prop)


def combine(ns, weight_ref, elem_ref, phi_ref):
    nop, _, rows, nv = elem_ref.shape
    span = weight_ref.shape[1] // nop
    shape = (span, nop * span)
    unit = lax.rem(lax.broadcasted_iota(jnp.int32, shape, 1), span) == lax.broadcasted_iota(jnp.int32, shape, 0)
    spread = jnp.concatenate(
        [jnp.where(unit, weight_ref[n : n + 1, :], 0.0).astype(BF16) for n in range(ns * ns)], axis=0
    )
    for c in range(2):
        for first in range(0, rows, span):
            parts = jnp.concatenate([elem_ref[o, c, first : first + span, :] for o in range(nop)], axis=0)
            total = jnp.dot(spread, parts, preferred_element_type=F32).astype(BF16)
            for n in range(ns * ns):
                row = n // ns * rows + first
                phi_ref[c, row : row + span, n % ns * nv : (n % ns + 1) * nv] = total[n * span : (n + 1) * span]


def tiles_of(stage):
    core = lax.axis_index("blk")
    side = lax.axis_index("pair") // (lax.axis_size("pair") // 2)
    swap = core ^ side
    if stage == "early":
        return (side, core), (side, 1 - core), (1 - side, swap), (1 - side, 1 - swap)
    return (side, swap), (side, 1 - swap), (1 - side, core), (1 - side, 1 - core)


def dress_kernel(ns, stage, *refs):
    weight_ref, elem_ref, own_ref, other_ref, *outs, phi = refs[:-2]
    held, arrived = refs[-2:]
    core = lax.axis_index("blk")
    loads = []
    for n, (s, c) in enumerate(tiles_of(stage)):
        pair = [
            pltpu.make_async_copy(ref.at[c * 2 + s], held.at[n, place], arrived.at[n, m])
            for m, (ref, place) in enumerate(((own_ref, core), (other_ref, 1 - core)))
        ]
        for load in pair:
            load.start()
        loads.append(pair)
    combine(ns, weight_ref, elem_ref, phi)
    width = held.shape[-1]
    dot = functools.partial(jnp.dot, preferred_element_type=F32)
    for n, out in enumerate(outs):
        for load in loads[n]:
            load.wait()
        prop_real, prop_imag = (
            jnp.concatenate([held[n, 0, c], held[n, 1, c]], axis=1) for c in range(2)
        )
        real = dot(phi[0], prop_real) - dot(phi[1], prop_imag)
        imag = dot(phi[0], prop_imag) + dot(phi[1], prop_real)
        for place in range(2):
            part = slice(place * width, (place + 1) * width)
            out[place, 0] = real[:, part].astype(BF16)
            out[place, 1] = imag[:, part].astype(BF16)


def dress(stage, weight, elem, own, other, ns):
    order, width = own.shape[2:]
    rows = ns * elem.shape[2]
    block = jax.ShapeDtypeStruct((2, 2, rows, width), BF16)
    return pl.pallas_call(
        functools.partial(dress_kernel, ns, stage),
        out_shape=[block] * 4,
        in_specs=[VMEM, VMEM, ANY, ANY],
        out_specs=[VMEM] * 4,
        scratch_shapes=[
            pltpu.VMEM((2, rows, order), BF16),
            pltpu.VMEM((4, 2, *own.shape[1:]), BF16),
            pltpu.SemaphoreType.DMA((4, 2)),
        ],
        cost_estimate=pl.CostEstimate(
            flops=64 * rows * order * width,
            bytes_accessed=32 * order * width,
            transcendentals=0,
        ),
        compiler_params=pltpu.CompilerParams(vmem_limit_bytes=16 * MIB),
    )(weight, elem, own, other)


def trace_kernel(mine_ref, theirs_ref, before_ref, out_ref):
    width = mine_ref.shape[-1]
    real = imag = None
    for block in range(2):
        span = slice(block * width, (block + 1) * width)
        left = [
            jnp.concatenate([mine_ref[0, c, span, :], mine_ref[1, c, span, :]], axis=1)
            for c in range(2)
        ]
        right = [theirs_ref[block, c] for c in range(2)]
        dot = functools.partial(jnp.dot, preferred_element_type=F32)
        re = dot(left[0], right[0]) - dot(left[1], right[1])
        im = dot(left[0], right[1]) + dot(left[1], right[0])
        real = re if real is None else real + re
        imag = im if imag is None else imag + im
    shape = real.shape
    diagonal = lax.broadcasted_iota(jnp.int32, shape, 0) == lax.broadcasted_iota(jnp.int32, shape, 1)
    real = jnp.sum(jnp.where(diagonal, real, 0.0))
    imag = jnp.sum(jnp.where(diagonal, imag, 0.0))
    lane = lax.broadcasted_iota(jnp.int32, out_ref.shape, 1)
    out_ref[...] = before_ref[...] + jnp.where(lane == 0, real, jnp.where(lane == 1, imag, 0.0))


def trace(mine, theirs, before):
    return pl.pallas_call(
        trace_kernel,
        out_shape=jax.ShapeDtypeStruct(before.shape, F32),
        in_specs=[VMEM] * 3,
        out_specs=VMEM,
        cost_estimate=pl.CostEstimate(
            flops=8 * mine.shape[2] ** 3, bytes_accessed=4 * mine.size, transcendentals=0
        ),
        compiler_params=pltpu.CompilerParams(vmem_limit_bytes=4 * MIB),
        name="trace",
    )(mine, theirs, before)


def shards(elementals, perambulator, pairs, elem_index, coef_code, term_count):
    peers = lax.axis_size("pair")
    half = peers // 2
    me = lax.axis_index("pair")
    nop, entries = elementals.shape[1], elementals.shape[-1]
    nterms, ns = elem_index.shape[1], coef_code.shape[-1]
    order, _ = perambulator.shape[2:]
    nv = order // ns
    rows = entries // nv

    def across(value, turn):
        moves = []
        for p in range(peers):
            for c in range(2):
                moves.append((p * 2 + c, (p + half) % peers * 2 + (c ^ turn[p // half])))
        return lax.ppermute(value, ("pair", "blk"), moves)

    def beside(value):
        return lax.ppermute(value, "blk", [(0, 1), (1, 0)])

    def within(value):
        groups = [list(range(half)), list(range(half, peers))]
        return lax.all_to_all(value, "pair", 0, 0, axis_index_groups=groups, tiled=True)

    def rows_of(received):
        shaped = received.reshape(half, nop, 2, rows, nv)
        return shaped.transpose(1, 2, 0, 3, 4).reshape(nop, 2, half * rows, nv)

    times = pairs.T
    away, home = pick(elementals, times, half)
    crossed = across(away, (0, 0))
    home = within(home)

    own = sort(half, rows, nv, perambulator[0])
    other = beside(own)

    used = jnp.arange(nterms) < term_count[me]
    weights = jnp.where(used[:, None, None], coef_code[me], 0)
    named = elem_index[me][None, :] == jnp.arange(nop)[:, None]
    weight = jnp.sum(jnp.where(named[:, :, None, None], weights[None], 0), axis=1)
    weight = (weight.astype(F32) * 0.5).reshape(nop, ns * ns).T
    weight = jnp.repeat(weight, nv // nop, axis=1)

    near, near_turned, mixed, mixed_kept = dress("early", weight, rows_of(home), own, other, ns)
    got_near = across(near, (0, 0))
    got_near_turned = across(near_turned, (1, 1))
    away = within(crossed)
    got_mixed = across(mixed, (0, 1))

    last, last_kept, far, far_turned = dress("late", weight, rows_of(away), own, other, ns)
    got_last = across(last, (0, 1))

    total = jnp.zeros((1, 2), F32)
    total = trace(far, got_near, total)
    total = trace(far_turned, got_near_turned, total)
    total = trace(mixed_kept, got_mixed, total)
    total = trace(last_kept, got_last, total)

    other = beside(total)
    there = across(total, (0, 0))
    return (total + there) + (other + beside(there))


def solution(mesh):
    return jax.shard_map(
        shards,
        mesh=mesh,
        in_specs=(
            P("cfg", None, None, ("pair", "blk")),
            P(("cfg", "pair"), None, None, "blk"),
            P(),
            P(),
            P(),
            P(),
        ),
        out_specs=P(("cfg", "pair"), None),
        check_vma=False,
    )
```

```python
import functools

import jax
import jax.numpy as jnp
from jax import lax
from jax.experimental import pallas as pl
from jax.experimental.pallas import tpu as pltpu
from jax.sharding import PartitionSpec as P


F32 = jnp.float32
BF16 = jnp.bfloat16
MIB = 1 << 20

ANY = pl.BlockSpec(memory_space=pl.ANY)
VMEM = pl.BlockSpec(memory_space=pltpu.VMEM)
SMEM = pl.BlockSpec(memory_space=pltpu.SMEM)


def pick_kernel(times_ref, table_ref, away_ref, home_ref, left):
    half = home_ref.shape[0]
    side = lax.axis_index("pair") // half
    stores = []
    for out, first in ((away_ref, (1 - side) * half), (home_ref, side * half)):
        for n in range(half):
            time = times_ref[0, first + n]
            stores.append(pltpu.make_async_copy(table_ref.at[time], out.at[n], left.at[len(stores)]))
    for store in stores:
        store.start()
    for store in stores:
        store.wait()


def pick(table, times, half):
    return pl.pallas_call(
        pick_kernel,
        out_shape=[jax.ShapeDtypeStruct((half, *table.shape[1:]), table.dtype)] * 2,
        in_specs=[SMEM, VMEM],
        out_specs=[ANY] * 2,
        scratch_shapes=[pltpu.SemaphoreType.DMA((2 * half,))],
        cost_estimate=pl.CostEstimate(
            flops=0, bytes_accessed=4 * table.size, transcendentals=0
        ),
        name="pick",
    )(times, table)


def sort_kernel(half, rows, nv, prop_ref, out_ref):
    columns = prop_ref.shape[-1]
    wide = columns // nv
    quarter = nv // 4
    source = lax.broadcasted_iota(jnp.int32, (columns, columns), 0)
    target = lax.broadcasted_iota(jnp.int32, (columns, columns), 1)
    place = lax.rem(target, quarter)
    b = lax.rem(target // quarter, wide)
    side = lax.rem(target // (quarter * wide), 2)
    core = target // (2 * quarter * wide)
    device = side * half + place // rows
    wanted = b * nv + (device * 2 + core) * rows + lax.rem(place, rows)
    order = jnp.where(source == wanted, 1.0, 0.0).astype(BF16)
    width = out_ref.shape[-1]
    for c in range(2):
        sorted_part = jnp.dot(prop_ref[c], order, preferred_element_type=F32).astype(BF16)
        for tile in range(4):
            out_ref[tile, c] = sorted_part[:, tile * width : (tile + 1) * width]


def sort(half, rows, nv, prop):
    _, order, columns = prop.shape
    return pl.pallas_call(
        functools.partial(sort_kernel, half, rows, nv),
        out_shape=jax.ShapeDtypeStruct((4, 2, order, columns // 4), BF16),
        in_specs=[VMEM],
        out_specs=VMEM,
        cost_estimate=pl.CostEstimate(
            flops=4 * order * columns**2, bytes_accessed=8 * order * columns, transcendentals=0
        ),
        name="sort",
    )(prop)


def combine(ns, weight_ref, elem_ref, phi_ref):
    nop, _, rows, nv = elem_ref.shape
    span = weight_ref.shape[1] // nop
    shape = (span, nop * span)
    unit = lax.rem(lax.broadcasted_iota(jnp.int32, shape, 1), span) == lax.broadcasted_iota(jnp.int32, shape, 0)
    spread = jnp.concatenate(
        [jnp.where(unit, weight_ref[n : n + 1, :], 0.0).astype(BF16) for n in range(ns * ns)], axis=0
    )
    for c in range(2):
        for first in range(0, rows, span):
            parts = jnp.concatenate([elem_ref[o, c, first : first + span, :] for o in range(nop)], axis=0)
            total = jnp.dot(spread, parts, preferred_element_type=F32).astype(BF16)
            for n in range(ns * ns):
                row = n // ns * rows + first
                phi_ref[c, row : row + span, n % ns * nv : (n % ns + 1) * nv] = total[n * span : (n + 1) * span]


def tiles_of(stage):
    core = lax.axis_index("blk")
    side = lax.axis_index("pair") // (lax.axis_size("pair") // 2)
    swap = core ^ side
    if stage == "early":
        return (side, core), (side, 1 - core), (1 - side, swap), (1 - side, 1 - swap)
    return (side, swap), (side, 1 - swap), (1 - side, core), (1 - side, 1 - core)


def dress_kernel(ns, stage, *refs):
    weight_ref, elem_ref, own_ref, other_ref, *outs, phi = refs[:-2]
    held, arrived = refs[-2:]
    core = lax.axis_index("blk")
    loads = []
    for n, (s, c) in enumerate(tiles_of(stage)):
        pair = [
            pltpu.make_async_copy(ref.at[c * 2 + s], held.at[n, place], arrived.at[n, m])
            for m, (ref, place) in enumerate(((own_ref, core), (other_ref, 1 - core)))
        ]
        for load in pair:
            load.start()
        loads.append(pair)
    combine(ns, weight_ref, elem_ref, phi)
    width = held.shape[-1]
    dot = functools.partial(jnp.dot, preferred_element_type=F32)
    for n in range(0, len(outs), 2):
        for load in (*loads[n], *loads[n + 1]):
            load.wait()
        prop_real, prop_imag = (
            jnp.concatenate([held[m, place, c] for m in (n, n + 1) for place in range(2)], axis=1)
            for c in range(2)
        )
        step = outs[n].shape[2] // 2
        for first in range(0, outs[n].shape[2], step):
            span = slice(first, first + step)
            real = dot(phi[0, span], prop_real) - dot(phi[1, span], prop_imag)
            imag = dot(phi[0, span], prop_imag) + dot(phi[1, span], prop_real)
            for m in range(4):
                part = slice(m * width, (m + 1) * width)
                out = outs[n + m // 2]
                out[m % 2, 0, span] = real[:, part].astype(BF16)
                out[m % 2, 1, span] = imag[:, part].astype(BF16)


def dress(stage, weight, elem, own, other, ns):
    order, width = own.shape[2:]
    rows = ns * elem.shape[2]
    block = jax.ShapeDtypeStruct((2, 2, rows, width), BF16)
    return pl.pallas_call(
        functools.partial(dress_kernel, ns, stage),
        out_shape=[block] * 4,
        in_specs=[VMEM, VMEM, ANY, ANY],
        out_specs=[VMEM] * 4,
        scratch_shapes=[
            pltpu.VMEM((2, rows, order), BF16),
            pltpu.VMEM((4, 2, *own.shape[1:]), BF16),
            pltpu.SemaphoreType.DMA((4, 2)),
        ],
        cost_estimate=pl.CostEstimate(
            flops=64 * rows * order * width,
            bytes_accessed=32 * order * width,
            transcendentals=0,
        ),
        compiler_params=pltpu.CompilerParams(vmem_limit_bytes=16 * MIB),
    )(weight, elem, own, other)


def trace_kernel(mine_ref, theirs_ref, before_ref, out_ref):
    width = mine_ref.shape[-1]
    left, right = ([], []), []
    for block in range(2):
        span = slice(block * width, (block + 1) * width)
        for c in range(2):
            left[c].extend(mine_ref[place, c, span, :] for place in range(2))
        right.append(jnp.concatenate([theirs_ref[block, c] for c in range(2)], axis=1))
    right = jnp.concatenate(right, axis=0)
    by_real, by_imag = (
        jnp.dot(jnp.concatenate(part, axis=1), right, preferred_element_type=F32) for part in left
    )
    real = by_real[:, :width] - by_imag[:, width:]
    imag = by_real[:, width:] + by_imag[:, :width]
    shape = real.shape
    diagonal = lax.broadcasted_iota(jnp.int32, shape, 0) == lax.broadcasted_iota(jnp.int32, shape, 1)
    real = jnp.sum(jnp.where(diagonal, real, 0.0))
    imag = jnp.sum(jnp.where(diagonal, imag, 0.0))
    lane = lax.broadcasted_iota(jnp.int32, out_ref.shape, 1)
    out_ref[...] = before_ref[...] + jnp.where(lane == 0, real, jnp.where(lane == 1, imag, 0.0))


def trace(mine, theirs, before):
    return pl.pallas_call(
        trace_kernel,
        out_shape=jax.ShapeDtypeStruct(before.shape, F32),
        in_specs=[VMEM] * 3,
        out_specs=VMEM,
        cost_estimate=pl.CostEstimate(
            flops=8 * mine.shape[2] ** 3, bytes_accessed=4 * mine.size, transcendentals=0
        ),
        compiler_params=pltpu.CompilerParams(vmem_limit_bytes=2 * MIB),
        name="trace",
    )(mine, theirs, before)


def shards(elementals, perambulator, pairs, elem_index, coef_code, term_count):
    peers = lax.axis_size("pair")
    half = peers // 2
    me = lax.axis_index("pair")
    nop, entries = elementals.shape[1], elementals.shape[-1]
    nterms, ns = elem_index.shape[1], coef_code.shape[-1]
    order, _ = perambulator.shape[2:]
    nv = order // ns
    rows = entries // nv

    def across(value, turn):
        moves = []
        for p in range(peers):
            for c in range(2):
                moves.append((p * 2 + c, (p + half) % peers * 2 + (c ^ turn[p // half])))
        return lax.ppermute(value, ("pair", "blk"), moves)

    def beside(value):
        return lax.ppermute(value, "blk", [(0, 1), (1, 0)])

    def within(value):
        groups = [list(range(half)), list(range(half, peers))]
        return lax.all_to_all(value, "pair", 0, 0, axis_index_groups=groups, tiled=True)

    def rows_of(received):
        shaped = received.reshape(half, nop, 2, rows, nv)
        return shaped.transpose(1, 2, 0, 3, 4).reshape(nop, 2, half * rows, nv)

    times = pairs.T
    away, home = pick(elementals, times, half)
    crossed = across(away, (0, 0))
    home = within(home)

    own = sort(half, rows, nv, perambulator[0])
    other = beside(own)

    used = jnp.arange(nterms) < term_count[me]
    weights = jnp.where(used[:, None, None], coef_code[me], 0)
    named = elem_index[me][None, :] == jnp.arange(nop)[:, None]
    weight = jnp.sum(jnp.where(named[:, :, None, None], weights[None], 0), axis=1)
    weight = (weight.astype(F32) * 0.5).reshape(nop, ns * ns).T
    weight = jnp.repeat(weight, nv // nop, axis=1)

    near, near_turned, mixed, mixed_kept = dress("early", weight, rows_of(home), own, other, ns)
    got_near = across(near, (0, 0))
    got_near_turned = across(near_turned, (1, 1))
    away = within(crossed)
    got_mixed = across(mixed, (0, 1))

    last, last_kept, far, far_turned = dress("late", weight, rows_of(away), own, other, ns)
    got_last = across(last, (0, 1))

    total = jnp.zeros((1, 2), F32)
    total = trace(far, got_near, total)
    total = trace(far_turned, got_near_turned, total)
    total = trace(mixed_kept, got_mixed, total)
    total = trace(last_kept, got_last, total)

    other = beside(total)
    there = across(total, (0, 0))
    return (total + there) + (other + beside(there))


def solution(mesh):
    return jax.shard_map(
        shards,
        mesh=mesh,
        in_specs=(
            P("cfg", None, None, ("pair", "blk")),
            P(("cfg", "pair"), None, None, "blk"),
            P(),
            P(),
            P(),
            P(),
        ),
        out_specs=P(("cfg", "pair"), None),
        check_vma=False,
    )
```

```python
import functools

import jax
import jax.numpy as jnp
from jax import lax
from jax.experimental import pallas as pl
from jax.experimental.pallas import tpu as pltpu
from jax.sharding import PartitionSpec as P


F32 = jnp.float32
BF16 = jnp.bfloat16
MIB = 1 << 20

ANY = pl.BlockSpec(memory_space=pl.ANY)
VMEM = pl.BlockSpec(memory_space=pltpu.VMEM)
SMEM = pl.BlockSpec(memory_space=pltpu.SMEM)


def pick_kernel(times_ref, table_ref, away_ref, home_ref, left):
    half = home_ref.shape[0]
    side = lax.axis_index("pair") // half
    stores = []
    for out, first in ((away_ref, (1 - side) * half), (home_ref, side * half)):
        for n in range(half):
            time = times_ref[0, first + n]
            stores.append(pltpu.make_async_copy(table_ref.at[time], out.at[n], left.at[len(stores)]))
    for store in stores:
        store.start()
    for store in stores:
        store.wait()


def pick(table, times, half):
    return pl.pallas_call(
        pick_kernel,
        out_shape=[jax.ShapeDtypeStruct((half, *table.shape[1:]), table.dtype)] * 2,
        in_specs=[SMEM, VMEM],
        out_specs=[ANY] * 2,
        scratch_shapes=[pltpu.SemaphoreType.DMA((2 * half,))],
        cost_estimate=pl.CostEstimate(
            flops=0, bytes_accessed=4 * table.size, transcendentals=0
        ),
        name="pick",
    )(times, table)


def sort_kernel(half, rows, nv, prop_ref, out_ref):
    columns = prop_ref.shape[-1]
    wide = columns // nv
    quarter = nv // 4
    source = lax.broadcasted_iota(jnp.int32, (columns, columns), 0)
    target = lax.broadcasted_iota(jnp.int32, (columns, columns), 1)
    place = lax.rem(target, quarter)
    b = lax.rem(target // quarter, wide)
    side = lax.rem(target // (quarter * wide), 2)
    core = target // (2 * quarter * wide)
    device = side * half + place // rows
    wanted = b * nv + (device * 2 + core) * rows + lax.rem(place, rows)
    order = jnp.where(source == wanted, 1.0, 0.0).astype(BF16)
    width = out_ref.shape[-1]
    for c in range(2):
        sorted_part = jnp.dot(prop_ref[c], order, preferred_element_type=F32).astype(BF16)
        for tile in range(4):
            out_ref[tile, c] = sorted_part[:, tile * width : (tile + 1) * width]


def sort(half, rows, nv, prop):
    _, order, columns = prop.shape
    return pl.pallas_call(
        functools.partial(sort_kernel, half, rows, nv),
        out_shape=jax.ShapeDtypeStruct((4, 2, order, columns // 4), BF16),
        in_specs=[VMEM],
        out_specs=VMEM,
        cost_estimate=pl.CostEstimate(
            flops=4 * order * columns**2, bytes_accessed=8 * order * columns, transcendentals=0
        ),
        name="sort",
    )(prop)


def combine(ns, weight_ref, elem_ref, phi_ref):
    nop, _, rows, nv = elem_ref.shape
    span = weight_ref.shape[1] // nop
    shape = (span, nop * span)
    unit = lax.rem(lax.broadcasted_iota(jnp.int32, shape, 1), span) == lax.broadcasted_iota(jnp.int32, shape, 0)
    spread = jnp.concatenate(
        [jnp.where(unit, weight_ref[n : n + 1, :], 0.0).astype(BF16) for n in range(ns * ns)], axis=0
    )
    for c in range(2):
        for first in range(0, rows, span):
            parts = jnp.concatenate([elem_ref[o, c, first : first + span, :] for o in range(nop)], axis=0)
            total = jnp.dot(spread, parts, preferred_element_type=F32).astype(BF16)
            for n in range(ns * ns):
                row = n // ns * rows + first
                phi_ref[c, row : row + span, n % ns * nv : (n % ns + 1) * nv] = total[n * span : (n + 1) * span]


def tiles_of(stage):
    core = lax.axis_index("blk")
    side = lax.axis_index("pair") // (lax.axis_size("pair") // 2)
    swap = core ^ side
    if stage == "early":
        return (side, core), (side, 1 - core), (1 - side, swap), (1 - side, 1 - swap)
    return (side, swap), (side, 1 - swap), (1 - side, core), (1 - side, 1 - core)


def dress_kernel(ns, stage, *refs):
    weight_ref, elem_ref, own_ref, other_ref, *outs, phi = refs[:-2]
    held, arrived = refs[-2:]
    core = lax.axis_index("blk")
    loads = []
    for n, (s, c) in enumerate(tiles_of(stage)):
        pair = [
            pltpu.make_async_copy(ref.at[c * 2 + s], held.at[n, place], arrived.at[n, m])
            for m, (ref, place) in enumerate(((own_ref, core), (other_ref, 1 - core)))
        ]
        for load in pair:
            load.start()
        loads.append(pair)
    combine(ns, weight_ref, elem_ref, phi)
    width = held.shape[-1]
    dot = functools.partial(jnp.dot, preferred_element_type=F32)
    for n in range(0, len(outs), 2):
        for load in (*loads[n], *loads[n + 1]):
            load.wait()
        prop_real, prop_imag = (
            jnp.concatenate([held[m, place, c] for m in (n, n + 1) for place in range(2)], axis=1)
            for c in range(2)
        )
        step = outs[n].shape[2] // 2
        for first in range(0, outs[n].shape[2], step):
            span = slice(first, first + step)
            real = dot(phi[0, span], prop_real) - dot(phi[1, span], prop_imag)
            imag = dot(phi[0, span], prop_imag) + dot(phi[1, span], prop_real)
            for m in range(4):
                part = slice(m * width, (m + 1) * width)
                out = outs[n + m // 2]
                out[m % 2, 0, span] = real[:, part].astype(BF16)
                out[m % 2, 1, span] = imag[:, part].astype(BF16)


def dress(stage, weight, elem, own, other, ns):
    order, width = own.shape[2:]
    rows = ns * elem.shape[2]
    block = jax.ShapeDtypeStruct((2, 2, rows, width), BF16)
    return pl.pallas_call(
        functools.partial(dress_kernel, ns, stage),
        out_shape=[block] * 4,
        in_specs=[VMEM, VMEM, ANY, ANY],
        out_specs=[VMEM] * 4,
        scratch_shapes=[
            pltpu.VMEM((2, rows, order), BF16),
            pltpu.VMEM((4, 2, *own.shape[1:]), BF16),
            pltpu.SemaphoreType.DMA((4, 2)),
        ],
        cost_estimate=pl.CostEstimate(
            flops=64 * rows * order * width,
            bytes_accessed=32 * order * width,
            transcendentals=0,
        ),
        compiler_params=pltpu.CompilerParams(vmem_limit_bytes=16 * MIB),
    )(weight, elem, own, other)


def trace_kernel(mine_ref, theirs_ref, before_ref, out_ref):
    width = mine_ref.shape[-1]
    real = imag = None
    for block in range(2):
        span = slice(block * width, (block + 1) * width)
        left = [
            jnp.concatenate([mine_ref[0, c, span, :], mine_ref[1, c, span, :]], axis=1)
            for c in range(2)
        ]
        right = [theirs_ref[block, c] for c in range(2)]
        dot = functools.partial(jnp.dot, preferred_element_type=F32)
        re = dot(left[0], right[0]) - dot(left[1], right[1])
        im = dot(left[0], right[1]) + dot(left[1], right[0])
        real = re if real is None else real + re
        imag = im if imag is None else imag + im
    shape = real.shape
    diagonal = lax.broadcasted_iota(jnp.int32, shape, 0) == lax.broadcasted_iota(jnp.int32, shape, 1)
    real = jnp.sum(jnp.where(diagonal, real, 0.0))
    imag = jnp.sum(jnp.where(diagonal, imag, 0.0))
    lane = lax.broadcasted_iota(jnp.int32, out_ref.shape, 1)
    out_ref[...] = before_ref[...] + jnp.where(lane == 0, real, jnp.where(lane == 1, imag, 0.0))


def trace(mine, theirs, before):
    return pl.pallas_call(
        trace_kernel,
        out_shape=jax.ShapeDtypeStruct(before.shape, F32),
        in_specs=[VMEM] * 3,
        out_specs=VMEM,
        cost_estimate=pl.CostEstimate(
            flops=8 * mine.shape[2] ** 3, bytes_accessed=4 * mine.size, transcendentals=0
        ),
        compiler_params=pltpu.CompilerParams(vmem_limit_bytes=2 * MIB),
        name="trace",
    )(mine, theirs, before)


def shards(elementals, perambulator, pairs, elem_index, coef_code, term_count):
    peers = lax.axis_size("pair")
    half = peers // 2
    me = lax.axis_index("pair")
    nop, entries = elementals.shape[1], elementals.shape[-1]
    nterms, ns = elem_index.shape[1], coef_code.shape[-1]
    order, _ = perambulator.shape[2:]
    nv = order // ns
    rows = entries // nv

    def across(value, turn):
        moves = []
        for p in range(peers):
            for c in range(2):
                moves.append((p * 2 + c, (p + half) % peers * 2 + (c ^ turn[p // half])))
        return lax.ppermute(value, ("pair", "blk"), moves)

    def beside(value):
        return lax.ppermute(value, "blk", [(0, 1), (1, 0)])

    def within(value):
        groups = [list(range(half)), list(range(half, peers))]
        return lax.all_to_all(value, "pair", 0, 0, axis_index_groups=groups, tiled=True)

    def rows_of(received):
        shaped = received.reshape(half, nop, 2, rows, nv)
        return shaped.transpose(1, 2, 0, 3, 4).reshape(nop, 2, half * rows, nv)

    times = pairs.T
    away, home = pick(elementals, times, half)
    crossed = across(away, (0, 0))
    home = within(home)

    own = sort(half, rows, nv, perambulator[0])
    other = beside(own)

    used = jnp.arange(nterms) < term_count[me]
    weights = jnp.where(used[:, None, None], coef_code[me], 0)
    named = elem_index[me][None, :] == jnp.arange(nop)[:, None]
    weight = jnp.sum(jnp.where(named[:, :, None, None], weights[None], 0), axis=1)
    weight = (weight.astype(F32) * 0.5).reshape(nop, ns * ns).T
    weight = jnp.repeat(weight, nv // nop, axis=1)

    near, near_turned, mixed, mixed_kept = dress("early", weight, rows_of(home), own, other, ns)
    got_near = across(near, (0, 0))
    got_near_turned = across(near_turned, (1, 1))
    away = within(crossed)
    got_mixed = across(mixed, (0, 1))

    last, last_kept, far, far_turned = dress("late", weight, rows_of(away), own, other, ns)
    got_last = across(last, (0, 1))

    total = jnp.zeros((1, 2), F32)
    total = trace(far, got_near, total)
    total = trace(far_turned, got_near_turned, total)
    total = trace(mixed_kept, got_mixed, total)
    total = trace(last_kept, got_last, total)

    other = beside(total)
    there = across(total, (0, 0))
    return (total + there) + (other + beside(there))


def solution(mesh):
    return jax.shard_map(
        shards,
        mesh=mesh,
        in_specs=(
            P("cfg", None, None, ("pair", "blk")),
            P(("cfg", "pair"), None, None, "blk"),
            P(),
            P(),
            P(),
            P(),
        ),
        out_specs=P(("cfg", "pair"), None),
        check_vma=False,
    )
```
